256 devices in a mesh: tok: 16 (over y, x), col: 16 (over z, core).
Axes of the slice: x: 4, y: 4, z: 8, core: 2. Of those that a mesh axis runs over, the one named last changes fastest.
Arguments:
- activations: bfloat16 [32768, 8192], P('tok', 'col'), may hold values from -60 to 60, as said below
- weight: bfloat16 [8192, 8192], P('tok', 'col'), may hold values from -6 to 6
- keep_mask: int32 [8192, 8192], P('tok', 'col'), may hold values from 0 to 1
Outputs:
- new_weight: bfloat16 [8192, 8192], P('tok', 'col')
The draws below stay inside these ranges and needn't reach their ends.
Inputs may be any that keep to these rules, and one draw needn't show every extreme that they name: activations of calibration tokens.
All inputs are finite; a program needn't handle non-finite values.
Results may differ from the reference program's by a relative error of at most 0.00115.
Values may be sent and summed in bfloat16 or wider, within the bound.
A program may use at most 64 MiB of HBM per device.

```python
import math
import jax
import jax.numpy as jnp
from jax import lax

C = 8192
R = 8192
B = 1024
ITERS = 4
TOKENS = 32768
N_COL = 16


def draw_activations(key, part):
    keys = jax.random.split(jax.random.fold_in(key, 11), 4)
    scales = jnp.exp(jax.random.uniform(keys[0], (C,), jnp.float32, 0.0, math.log(10.0)))
    latent = jax.random.normal(keys[1], (TOKENS, 4), jnp.float32)
    loading = jax.random.normal(keys[2], (4, C), jnp.float32)
    noise = jax.random.normal(keys[3], (TOKENS, C), jnp.float32)
    share = 0.2
    values = scales[None, :] * (noise + share * jnp.dot(latent, loading))
    return jnp.clip(values, -60.0, 60.0).astype(jnp.bfloat16)


def with_ends(result, key, least, top_value):
    shape = result.shape
    place = [jax.random.randint(jax.random.fold_in(key, axis), (), 0, shape[axis]) for axis in range(len(shape))]
    result = result.at[tuple(place)].set(least)
    longest = shape.index(max(shape))
    place[longest] = (place[longest] + 1) % shape[longest]
    return result.at[tuple(place)].set(top_value)


def level_of(key, dims, cuts, least, largest):
    def one(dim, parts):
        draws = jax.random.uniform(jax.random.fold_in(jax.random.fold_in(key, 6), dim), (parts,), jnp.float32, least / len(cuts), largest / len(cuts))
        return jnp.repeat(jnp.exp(draws), dims[dim] // parts).reshape((-1,) + (1,) * (len(dims) - dim - 1))

    loudness = one(*cuts[0])
    for cut in cuts[1:]:
        loudness = loudness * one(*cut)
    return loudness


def normal_values(rng, extent, deviation, reach, pieces=(), held_as=jnp.bfloat16):
    level = level_of(rng, extent, pieces, -0.22, 0.18) if pieces else 1.0
    entries = jax.random.normal(rng, extent, jnp.float32) * deviation * level
    return jnp.minimum(jnp.maximum(entries, -reach), reach).astype(held_as)


def setup_inputs(seed: int = 0) -> dict:
    seeds = jax.random.split(jax.random.key(seed), 4)
    activations = draw_activations(jax.random.fold_in(seeds[3], 71), 0)
    weight = normal_values(seeds[1], (R, C), 1.0, 6.0, ((0, 16), (1, 16)))
    keep_mask = with_ends(jax.random.randint(seeds[2], (R, C), 0, 2), jax.random.fold_in(seeds[2], 1), 0, 1).astype(jnp.int32)
    return dict(activations=activations, weight=weight, keep_mask=keep_mask)


def reference(activations, weight, keep_mask):
    highest = lax.Precision.HIGHEST
    total_tokens = activations.shape[0]
    columns = weight.shape[1]
    col_width = columns // N_COL
    panel_width = B // N_COL
    slots = jnp.arange(B, dtype=jnp.int32)
    panel_ids = (slots // panel_width * col_width + slots % panel_width).astype(jnp.int32)
    widened = activations.astype(jnp.float32)
    selected = jnp.take(widened, panel_ids, axis=1)
    hessian_panel = jnp.dot(widened.T, selected, precision=highest) / total_tokens
    block = jnp.take(hessian_panel, panel_ids, axis=0)
    identity = jnp.eye(B, dtype=jnp.float32)
    damped = block + 0.01 * jnp.mean(jnp.diagonal(block)) * identity
    iterate = identity / jnp.sqrt(jnp.sum(damped * damped))
    for sweep in range(ITERS):
        product = jnp.dot(iterate, damped, precision=highest)
        iterate = 2.0 * iterate - jnp.dot(product, iterate, precision=highest)
    pruned = weight.astype(jnp.float32) * (1 - keep_mask).astype(jnp.float32)
    pruned_panel = jnp.take(pruned, panel_ids, axis=1)
    factor = jnp.dot(pruned_panel, iterate, precision=highest)
    correction = jnp.dot(factor, hessian_panel.T, precision=highest)
    kept = keep_mask.astype(jnp.float32)
    return (kept * (weight.astype(jnp.float32) - correction)).astype(jnp.bfloat16)
```

```python
import jax
import jax.numpy as jnp
from jax import lax
from jax.sharding import PartitionSpec as P

B = 1024
ITERS = 4


def split(x):
    high = lax.reduce_precision(x, exponent_bits=8, mantissa_bits=7)
    return high.astype(jnp.bfloat16), (x - high).astype(jnp.bfloat16)


def mm(a, b, dims=(((1,), (0,)), ((), ()))):
    return lax.dot_general(a, b, dims, preferred_element_type=jnp.float32)


def per_device(activations, weight, keep_mask):
    n_col = lax.axis_size("col")
    n_tok = lax.axis_size("tok")
    tok_rows = activations.shape[0]
    panel_width = B // n_col
    total_count = tok_rows * n_tok
    pruned = jnp.where(
        keep_mask[:, :panel_width] == 0, weight[:, :panel_width], jnp.zeros((), jnp.bfloat16)
    )
    panel = lax.all_gather(activations[:, :panel_width], "col", axis=1, tiled=True)
    partial_panel = mm(activations, panel, (((0,), (0,)), ((), ())))
    pruned_panel = lax.all_gather(pruned, "col", axis=1, tiled=True)
    hessian_panel = lax.psum(partial_panel, "tok") / total_count
    block = lax.all_gather(hessian_panel[:panel_width], "col", axis=0, tiled=True)
    rows = lax.broadcasted_iota(jnp.int32, (B, B), 0)
    columns = lax.broadcasted_iota(jnp.int32, (B, B), 1)
    on_diagonal = rows == columns
    mean_diagonal = jnp.sum(jnp.where(on_diagonal, block, 0.0)) / B
    damped = block + jnp.where(on_diagonal, 0.01 * mean_diagonal, 0.0)
    scale = lax.rsqrt(jnp.sum(damped * damped))
    g = damped * scale
    y = pruned_panel.astype(jnp.float32)
    for sweep in range(ITERS):
        g_high = g.astype(jnp.bfloat16)
        y_high, y_low = split(y)
        y = 2.0 * y - (mm(y_high, g_high) + mm(y_low, g_high))
        if sweep < ITERS - 1:
            g = 2.0 * g - mm(g_high, g_high)
    y_high, y_low = split(y * scale)
    h_high, h_low = split(hessian_panel)
    nt = (((1,), (1,)), ((), ()))
    correction = mm(y_high, h_high, nt) + mm(y_low, h_high, nt) + mm(y_high, h_low, nt)
    kept = keep_mask.astype(jnp.float32)
    return (kept * (weight.astype(jnp.float32) - correction)).astype(jnp.bfloat16)


def solution(mesh):
    return jax.shard_map(
        per_device,
        mesh=mesh,
        in_specs=(P("tok", "col"), P("tok", "col"), P("tok", "col")),
        out_specs=P("tok", "col"),
        check_vma=False,
    )
```

```python
import functools

import jax
import jax.numpy as jnp
from jax import lax
from jax.experimental import pallas as pl
from jax.experimental.pallas import tpu as pltpu
from jax.sharding import PartitionSpec as P

B = 1024
ITERS = 4
NZ, NY, NX, NT, NQ = 8, 4, 4, 16, 16
WIDTH = 64
OFFSETS = (0, -1, 1, -2, 2, -3, 3, 4)
GROUPS = ((0, 1), (1, 2), (3, 2), (5, 2), (7, 1))
BF, F32 = jnp.bfloat16, jnp.float32


def dot(a, b):
    return jnp.dot(a, b, preferred_element_type=F32)


def hop(d, k, v):
    return d * 7 + (k - 1) * 2 + (v if k < 4 else 0)


def units(d, k):
    return (0, 1) if k < 4 else (d,)


def kernel(
    a_hbm, w_hbm, m_hbm, out_ref,
    a, w, m, pt, hts, rsr, red, dsend, drecv, dzs, drho, g, gb, hta, hh, hl, pts, pall, y, yb, yx,
    load_sem, sib_s, sib_r, ring_s, ring_r, fwd_s, fwd_r, rs_s, rs_r, dsib_s, dsib_r, dz_s, dz_r,
    dxy_s, dxy_r, df_s, df_r, pz_s, pz_r, ha_s, ha_r, yx_s, yx_r,
):
    t, q = lax.axis_index("tok"), lax.axis_index("col")
    ty, tx = lax.div(t, NX), lax.rem(t, NX)
    z, c = lax.div(q, 2), lax.rem(q, 2)
    other = 1 - c
    sibling = 2 * z + other
    inverse_count = 1.0 / (a.shape[0] * NT)

    def send(src, dst, send_sem, recv_sem, tok, col):
        pltpu.make_async_remote_copy(
            src_ref=src, dst_ref=dst, send_sem=send_sem, recv_sem=recv_sem,
            device_id=(tok, col), device_id_type=pl.DeviceIdType.MESH,
        ).start()

    def wait(ref, sem):
        pltpu.make_async_copy(ref, ref, sem).wait()

    def each(first, last, body):
        def step(i, carry):
            body(i)
            return carry
        lax.fori_loop(first, last, step, 0)

    loads = [
        pltpu.make_async_copy(a_hbm.at[:, 0:128], a.at[:, 0:128], load_sem.at[0]),
        pltpu.make_async_copy(a_hbm.at[:, 128:512], a.at[:, 128:512], load_sem.at[1]),
        pltpu.make_async_copy(w_hbm, w, load_sem.at[2]),
        pltpu.make_async_copy(m_hbm, m, load_sem.at[3]),
    ]
    for load in loads:
        load.start()

    barrier = pltpu.get_barrier_semaphore()

    def greet(i):
        pl.semaphore_signal(
            barrier, inc=1, device_id=(lax.rem(t + i, NT), q), device_id_type=pl.DeviceIdType.MESH
        )
        pl.semaphore_signal(
            barrier, inc=1, device_id=(t, lax.rem(q + i, NQ)), device_id_type=pl.DeviceIdType.MESH
        )

    each(1, 16, greet)

    loads[0].wait()
    for half in range(2):
        for part in range(2):
            rows = half * 1024 + part * 512
            piece = a[rows:rows + 512, 0:128].astype(F32).T
            pt[z, half, c, :, part * 512:(part + 1) * 512] = piece[0:WIDTH].astype(BF)
    pl.semaphore_wait(barrier, 30)

    def ring(d, k, v, origin):
        u = c if v == 0 else other
        ref = pt.at[origin, c, u]
        to = lax.rem(z + (1 if d == 0 else NZ - 1), NZ)
        send(ref, ref, ring_s.at[hop(d, k, v)], ring_r.at[hop(d, k, v)], t, 2 * to + c)

    send(pt.at[z, other, c], pt.at[z, other, c], sib_s.at[0], sib_r.at[0], t, sibling)
    ring(0, 1, 0, z)
    ring(1, 1, 0, z)
    send(pt.at[z, c, c], pt.at[z, c, c], sib_s.at[1], sib_r.at[1], t, sibling)
    wait(pt.at[z, c, other], sib_r.at[0])
    ring(0, 1, 1, z)
    ring(1, 1, 1, z)

    loads[2].wait()
    loads[3].wait()
    pruned = jnp.where(m[:, 0:128] == 0, w[:, 0:128].astype(F32), 0.0).T
    pts[0] = pruned[0:WIDTH, 0:256].astype(BF)
    pts[1] = pruned[0:WIDTH, 256:512].astype(BF)
    pall[q] = pts[c]

    loads[1].wait()
    wait(pt.at[z, other, other], sib_r.at[1])

    def chunk_at(slot):
        return lax.rem(z + OFFSETS[slot] + NZ, NZ)

    def partial_panel(group):
        first, n = GROUPS[group]
        total = None
        for half in range(2):
            lhs = [pt[chunk_at(first + i), half].reshape(128, 1024) for i in range(n)]
            lhs = lhs[0] if n == 1 else jnp.concatenate(lhs, axis=0)
            term = dot(lhs, a[half * 1024:(half + 1) * 1024, :])
            total = term if total is None else total + term
        for i in range(n):
            hts[:, first + i] = total[128 * i:128 * (i + 1)].reshape(16, 8, 512)
        rsr[t, first:first + n] = hts[t, first:first + n]

        def share(i):
            to = lax.rem(t + i, NT)
            send(
                hts.at[to, first:first + n], rsr.at[t, first:first + n],
                rs_s.at[group], rs_r.at[group], to, q,
            )

        each(1, 16, share)

    def reduce_group(group):
        first, n = GROUPS[group]
        wait(rsr.at[0:15, first:first + n], rs_r.at[group])
        for i in range(n):
            total = rsr[0, first + i]
            for source in range(1, NT):
                total = total + rsr[source, first + i]
            red[chunk_at(first + i)] = total * inverse_count

    partial_panel(0)
    for k in range(1, 5):
        for v in range(2):
            for d in range(2):
                if v not in units(d, k):
                    continue
                origin = lax.rem(z + (NZ - k if d == 0 else k), NZ)
                u = c if v == 0 else other
                ref = pt.at[origin, c, u]
                wait(ref, ring_r.at[hop(d, k, v)])
                if k < 4 and v in units(d, k + 1):
                    ring(d, k + 1, v, origin)
                send(ref, ref, fwd_s.at[hop(d, k, v)], fwd_r.at[hop(d, k, v)], t, sibling)
        for v in range(2):
            for d in range(2):
                if v in units(d, k):
                    origin = lax.rem(z + (NZ - k if d == 0 else k), NZ)
                    wait(pt.at[origin, other, other if v == 0 else c], fwd_r.at[hop(d, k, v)])
        partial_panel(k)
        if k >= 2:
            reduce_group(k - 2)
    reduce_group(3)
    reduce_group(4)

    lanes = lax.broadcasted_iota(jnp.int32, (64, 128), 1)
    own = red[:, :, 0:128].reshape(64, 128)
    own = jnp.where(c == 0, own, pltpu.roll(own, 64, 1))
    own = jnp.where(lax.div(lanes, 64) == c, own, 0.0)
    dsend[0] = own[0:32].astype(BF)
    dsend[1] = own[32:64].astype(BF)
    send(dsend.at[other], drecv, dsib_s.at[0], dsib_r.at[0], t, sibling)
    hta[:, ty, tx] = red[...]
    wait(drecv, dsib_r.at[0])
    here = (dsend[c].astype(F32) + drecv[...].astype(F32)).astype(BF).reshape(2, 16, 128)
    dzs[...] = here
    my_lanes = pl.ds(pl.multiple_of(z * 128, 128), 128)
    drho[ty, tx, c, :, :, my_lanes] = here

    def along_z(i):
        send(
            dzs, drho.at[ty, tx, c, :, :, my_lanes], dz_s.at[0], dz_r.at[0],
            t, 2 * lax.rem(z + i, NZ) + c,
        )

    each(1, NZ, along_z)

    def share_pruned(i):
        to = lax.rem(q + i, NQ)
        send(pts.at[lax.rem(to, 2)], pall.at[q], pz_s.at[0], pz_r.at[0], t, to)

    each(1, NQ, share_pruned)

    wait(drho.at[ty, tx, c, :, :, 0:896], dz_r.at[0])

    def along_x(i):
        return NX * ty + lax.rem(tx + i, NX)

    def along_y(i):
        return NX * lax.rem(ty + i, NY) + tx

    for i in range(1, 4):
        ref = drho.at[ty, tx, c, 0]
        send(ref, ref, dxy_s.at[0], dxy_r.at[0], along_x(i), q)
        ref = drho.at[ty, tx, c, 1]
        send(ref, ref, dxy_s.at[1], dxy_r.at[1], along_y(i), q)
    wait(drho.at[0, 0:3, c, 0], dxy_r.at[0])
    for i in range(1, 4):
        ref = drho.at[ty, :, c, 0]
        send(ref, ref, dxy_s.at[2], dxy_r.at[2], along_y(i), q)
    wait(drho.at[0, 0:3, c, 1], dxy_r.at[1])
    for i in range(1, 4):
        ref = drho.at[:, tx, c, 1]
        send(ref, ref, dxy_s.at[3], dxy_r.at[3], along_x(i), q)
    ref = drho.at[ty, :, c, 0]
    send(ref, ref, df_s.at[0], df_r.at[0], t, sibling)
    ref = drho.at[:, tx, c, 1]
    send(ref, ref, df_s.at[1], df_r.at[1], t, sibling)

    for i in range(1, 4):
        ref = hta.at[0:4, ty, tx]
        send(ref, ref, ha_s.at[0], ha_r.at[0], along_x(i), q)
        ref = hta.at[4:8, ty, tx]
        send(ref, ref, ha_s.at[1], ha_r.at[1], along_y(i), q)

    wait(pall.at[0:15], pz_r.at[0])
    for i in range(8):
        piece = pall[2 * i:2 * i + 2].reshape(128, 256).astype(F32).T
        y[:, 128 * i:128 * (i + 1)] = piece
        yb[0, 0:256, 128 * i:128 * (i + 1)] = piece.astype(BF)

    wait(drho.at[0:3, :, c, 0], dxy_r.at[2])
    for i in range(1, 4):
        ref = drho.at[lax.rem(ty + i, NY), :, c, 0]
        send(ref, ref, df_s.at[2], df_r.at[2], t, sibling)
    wait(drho.at[0:3, :, c, 1], dxy_r.at[3])
    for i in range(1, 4):
        ref = drho.at[:, lax.rem(tx + i, NX), c, 1]
        send(ref, ref, df_s.at[3], df_r.at[3], t, sibling)
    wait(drho.at[0, :, other, 0], df_r.at[0])
    wait(drho.at[0, :, other, 1], df_r.at[1])
    wait(drho.at[0:3, :, other, 0], df_r.at[2])
    wait(drho.at[0:3, :, other, 1], df_r.at[3])

    lane = lax.broadcasted_iota(jnp.int32, (8, 128), 1)
    row = lax.broadcasted_iota(jnp.int32, (8, 128), 0)

    def unpack(i, carry):
        squares, diagonal = carry
        block = drho[lax.div(i, NX), lax.rem(i, NX)].reshape(64, 1024).astype(F32).reshape(8, 8, 1024)
        g[:, i] = block
        on = lane == 8 * i + row
        for zo in range(NZ):
            squares = squares + block[zo] * block[zo]
            diagonal = diagonal + jnp.where(on, block[zo][:, 128 * zo:128 * (zo + 1)], 0.0)
        return squares, diagonal

    squares, diagonal = lax.fori_loop(
        0, NT, unpack, (jnp.zeros((8, 1024), F32), jnp.zeros((8, 128), F32))
    )
    trace = jnp.sum(diagonal, axis=(0, 1), keepdims=True)
    damping = trace * (0.01 / B)
    norm = jnp.sum(squares, axis=(0, 1), keepdims=True) + damping * (2.0 * trace + B * damping)
    scale = 1.0 / jnp.sqrt(norm)

    def damp(i):
        on = lane == 8 * i + row
        for zo in range(NZ):
            at = g[zo, i, :, 128 * zo:128 * (zo + 1)]
            g[zo, i, :, 128 * zo:128 * (zo + 1)] = at + jnp.where(on, damping, 0.0)

    each(0, NT, damp)

    def operand(i):
        gb[0, pl.ds(pl.multiple_of(i * 128, 128), 128), :] = g[i].reshape(128, 1024).astype(BF)

    each(0, NZ, operand)

    wait(hta.at[0:4, 0, 0:3], ha_r.at[0])
    wait(hta.at[4:8, 0, 0:3], ha_r.at[1])
    for i in range(1, 4):
        ref = hta.at[0:4, ty]
        send(ref, ref, ha_s.at[2], ha_r.at[2], along_y(i), q)
        ref = hta.at[4:8, :, tx]
        send(ref, ref, ha_s.at[3], ha_r.at[3], along_x(i), q)

    for k in range(ITERS - 1):
        def square(i):
            rows = pl.ds(pl.multiple_of(i * 256, 256), 256)
            product = dot(gb[k, rows, :], gb[k])
            old = g[pl.ds(2 * i, 2)].reshape(256, 1024)
            if k == 0:
                new = (2.0 * scale) * old - (scale * scale) * product
            else:
                new = 2.0 * old - product
            if k < ITERS - 2:
                g[pl.ds(2 * i, 2)] = new.reshape(2, 16, 8, 1024)
            gb[k + 1, rows, :] = new.astype(BF)

        each(0, 4, square)

    for k in range(ITERS):
        def apply(i):
            columns = pl.ds(pl.multiple_of(i * 256, 256), 256)
            if k == 0:
                step = scale * dot(yb[0, 0:256], gb[0, :, columns])
            else:
                both = dot(yb[k % 2], gb[k, :, columns])
                step = both[0:256] + both[256:512]
            new = 2.0 * y[:, columns] - step
            if k == ITERS - 1:
                new = new * scale
            high = new.astype(BF)
            low = (new - high.astype(F32)).astype(BF)
            if k < ITERS - 1:
                y[:, columns] = new
                yb[(k + 1) % 2, 0:256, columns] = high
                yb[(k + 1) % 2, 256:512, columns] = low
            else:
                yx[c, 0:256, columns] = high
                yx[c, 256:512, columns] = low

        each(0, 4, apply)

    send(yx.at[c], yx.at[c], yx_s.at[0], yx_r.at[0], t, sibling)

    wait(hta.at[0:4, 0:3], ha_r.at[2])
    wait(hta.at[4:8, 0:3], ha_r.at[3])
    for zo in range(NZ):
        block = hta[zo].reshape(128, 512)
        high = block.astype(BF)
        hh[128 * zo:128 * (zo + 1), :] = high
        hl[128 * zo:128 * (zo + 1), :] = (block - high.astype(F32)).astype(BF)

    def finish(part):
        rows = pl.ds(pl.multiple_of(part * 256, 256), 256)
        both = dot(yx[part], hh[...])
        correction = both[0:256] + both[256:512] + dot(yx[part, 0:256], hl[...])
        kept = m[rows, :].astype(F32)
        out_ref[rows, :] = (kept * (w[rows, :].astype(F32) - correction)).astype(BF)

    finish(c)
    wait(yx.at[other], yx_r.at[0])
    finish(other)

    wait(pt.at[z, other, c], sib_s.at[0])
    wait(pt.at[z, c, c], sib_s.at[1])
    for d in range(2):
        for k in range(1, 5):
            for v in units(d, k):
                wait(pt.at[z, c, c], ring_s.at[hop(d, k, v)])
                wait(pt.at[z, c, c], fwd_s.at[hop(d, k, v)])
    for group in range(5):
        first, n = GROUPS[group]
        wait(hts.at[0:15, first:first + n], rs_s.at[group])
    wait(dsend.at[other], dsib_s.at[0])
    wait(drho.at[ty, tx, c, :, :, 0:896], dz_s.at[0])
    wait(pall.at[0:15], pz_s.at[0])
    wait(drho.at[0, 0:3, c, 0], dxy_s.at[0])
    wait(drho.at[0, 0:3, c, 1], dxy_s.at[1])
    wait(drho.at[0:3, :, c, 0], dxy_s.at[2])
    wait(drho.at[0:3, :, c, 1], dxy_s.at[3])
    wait(drho.at[0, :, c, 0], df_s.at[0])
    wait(drho.at[0, :, c, 1], df_s.at[1])
    wait(drho.at[0:3, :, c, 0], df_s.at[2])
    wait(drho.at[0:3, :, c, 1], df_s.at[3])
    wait(hta.at[0:4, 0, 0:3], ha_s.at[0])
    wait(hta.at[4:8, 0, 0:3], ha_s.at[1])
    wait(hta.at[0:4, 0:3], ha_s.at[2])
    wait(hta.at[4:8, 0:3], ha_s.at[3])
    wait(yx.at[c], yx_s.at[0])


def per_device(activations, weight, keep_mask):
    sems = (4, 2, 2, 14, 14, 14, 14, 5, 5, 1, 1, 1, 1, 4, 4, 4, 4, 1, 1, 4, 4, 1, 1)
    return pl.pallas_call(
        kernel,
        out_shape=jax.ShapeDtypeStruct(weight.shape, BF),
        in_specs=[pl.BlockSpec(memory_space=pl.ANY)] * 3,
        out_specs=pl.BlockSpec(memory_space=pltpu.VMEM),
        scratch_shapes=[
            pltpu.VMEM((2048, 512), BF),
            pltpu.VMEM((512, 512), BF),
            pltpu.VMEM((512, 512), jnp.int32),
            pltpu.VMEM((NZ, 2, 2, WIDTH, 1024), BF),
            pltpu.VMEM((NT, 8, 8, 512), F32),
            pltpu.VMEM((NT, 8, 8, 512), F32),
            pltpu.VMEM((NZ, 8, 512), F32),
            pltpu.VMEM((2, 32, 128), BF),
            pltpu.VMEM((32, 128), BF),
            pltpu.VMEM((2, 16, 128), BF),
            pltpu.VMEM((NY, NX, 2, 2, 16, 1024), BF),
            pltpu.VMEM((NZ, NT, 8, 1024), F32),
            pltpu.VMEM((ITERS, 1024, 1024), BF),
            pltpu.VMEM((NZ, NY, NX, 8, 512), F32),
            pltpu.VMEM((1024, 512), BF),
            pltpu.VMEM((1024, 512), BF),
            pltpu.VMEM((2, WIDTH, 256), BF),
            pltpu.VMEM((NQ, WIDTH, 256), BF),
            pltpu.VMEM((256, 1024), F32),
            pltpu.VMEM((2, 512, 1024), BF),
            pltpu.VMEM((2, 512, 1024), BF),
        ] + [pltpu.SemaphoreType.DMA((n,)) for n in sems],
        compiler_params=pltpu.CompilerParams(
            collective_id=0, has_side_effects=True, vmem_limit_bytes=56 << 20
        ),
    )(activations, weight, keep_mask)


def solution(mesh):
    return jax.shard_map(
        per_device,
        mesh=mesh,
        in_specs=(P("tok", "col"), P("tok", "col"), P("tok", "col")),
        out_specs=P("tok", "col"),
        check_vma=False,
    )
```

```python
import functools

import jax
import jax.numpy as jnp
from jax import lax
from jax.experimental import pallas as pl
from jax.experimental.pallas import tpu as pltpu
from jax.sharding import PartitionSpec as P

B = 1024
ITERS = 4
NZ, NY, NX, NT, NQ = 8, 4, 4, 16, 16
WIDTH = 64
OFFSETS = (0, -1, 1, -2, 2, -3, 3, 4)
GROUPS = ((0, 1), (7, 1), (5, 2), (3, 2), (1, 2))
EARLY = (slice(0, 2), slice(2, 4))
PAIRS = ((1, 2), (3, 4), (5, 6), (0, 7))
BATCHES = (slice(5, 8), slice(0, 5))
BF, F32 = jnp.bfloat16, jnp.float32


def dot(a, b):
    return jnp.dot(a, b, preferred_element_type=F32)


def kernel(
    a_hbm, w_hbm, m_hbm, out_ref,
    a, w, m, pt, hts, ks, kr, r1, p1, r2, red, dn, dsend, drecv, dzs, drho, g, gb, hta, hh, hl, pts, pall, y, yb, yx,
    load_sem, sib_s, sib_r, ring_s, ring_r, fwd_s, fwd_r, rs_s, rs_r, r1_s, r1_r, r2_s, r2_r, dsib_s, dsib_r, dz_s, dz_r,
    dxy_s, dxy_r, df_s, df_r, pz_s, pz_r, ha_s, ha_r, yx_s, yx_r,
):
    t, q = lax.axis_index("tok"), lax.axis_index("col")
    ty, tx = lax.div(t, NX), lax.rem(t, NX)
    z, c = lax.div(q, 2), lax.rem(q, 2)
    other = 1 - c
    sibling = 2 * z + other
    inverse_count = 1.0 / (a.shape[0] * NT)

    def send(src, dst, send_sem, recv_sem, tok, col):
        pltpu.make_async_remote_copy(
            src_ref=src, dst_ref=dst, send_sem=send_sem, recv_sem=recv_sem,
            device_id=(tok, col), device_id_type=pl.DeviceIdType.MESH,
        ).start()

    def wait(ref, sem):
        pltpu.make_async_copy(ref, ref, sem).wait()

    def each(first, last, body):
        def step(i, carry):
            body(i)
            return carry
        lax.fori_loop(first, last, step, 0)

    loads = [
        pltpu.make_async_copy(a_hbm.at[:, 0:128], a.at[:, 0:128], load_sem.at[0]),
        pltpu.make_async_copy(a_hbm.at[:, 128:512], a.at[:, 128:512], load_sem.at[1]),
        pltpu.make_async_copy(w_hbm, w, load_sem.at[2]),
        pltpu.make_async_copy(m_hbm, m, load_sem.at[3]),
    ]
    for load in loads:
        load.start()

    barrier = pltpu.get_barrier_semaphore()

    def greet(i):
        pl.semaphore_signal(
            barrier, inc=1, device_id=(lax.rem(t + i, NT), q), device_id_type=pl.DeviceIdType.MESH
        )
        pl.semaphore_signal(
            barrier, inc=1, device_id=(t, lax.rem(q + i, NQ)), device_id_type=pl.DeviceIdType.MESH
        )

    each(1, 16, greet)

    loads[0].wait()
    for half in range(2):
        for part in range(2):
            rows = half * 1024 + part * 512
            piece = a[rows:rows + 512, 0:128].astype(F32).T
            pt[z, half, c, :, part * 512:(part + 1) * 512] = piece[0:WIDTH].astype(BF)
    pl.semaphore_wait(barrier, 30)

    following = lax.rem(z + NZ + 1 - 2 * c, NZ)

    def origin(k, core):
        return lax.rem(z + NZ + (2 * core - 1) * k, NZ)

    def ring(k, v):
        u = c if v < 2 else other
        ref = pt.at[origin(k - 1, c), c, u, 32 * (v % 2):32 * (v % 2) + 32]
        at = 4 * (k - 1) + v
        send(ref, ref, ring_s.at[at], ring_r.at[at], t, 2 * following + c)

    send(pt.at[z, other, c], pt.at[z, other, c], sib_s.at[0], sib_r.at[0], t, sibling)
    ring(1, 0)
    ring(1, 1)
    send(pt.at[z, c, c], pt.at[z, c, c], sib_s.at[1], sib_r.at[1], t, sibling)
    wait(pt.at[z, c, other], sib_r.at[0])
    ring(1, 2)
    ring(1, 3)

    loads[2].wait()
    loads[3].wait()
    pruned = jnp.where(m[:, 0:128] == 0, w[:, 0:128].astype(F32), 0.0).T
    pts[0] = pruned[0:WIDTH, 0:256].astype(BF)
    pts[1] = pruned[0:WIDTH, 256:512].astype(BF)
    pall[q] = pts[c]

    loads[1].wait()
    wait(pt.at[z, other, other], sib_r.at[1])

    def along_x(i):
        return NX * ty + lax.rem(tx + i, NX)

    def along_y(i):
        return NX * lax.rem(ty + i, NY) + tx

    def chunk_at(slot):
        return lax.rem(z + OFFSETS[slot] + NZ, NZ)

    def product(chunk, half):
        rows = pt[chunk, half].reshape(128, 1024)
        return dot(rows, a[1024 * half:1024 * (half + 1), :])

    def pass_on(k):
        for v in range(4):
            u = c if v < 2 else other
            wait(
                pt.at[origin(k, c), c, u, 32 * (v % 2):32 * (v % 2) + 32], ring_r.at[4 * (k - 1) + v]
            )
            if k < 7:
                ring(k + 1, v)
            if v % 2 == 1:
                ref = pt.at[origin(k, c), c, u]
                at = 2 * (k - 1) + v // 2
                send(ref, ref, fwd_s.at[at], fwd_r.at[at], t, sibling)

    def side_by_side(left, right):
        lanes = lax.broadcasted_iota(jnp.int32, (128, 128), 1)
        packed = jnp.where(lanes < WIDTH, left[:, 0:128], pltpu.roll(right[:, 0:128], WIDTH, 1))
        return packed.reshape(NY, NX, 8, 128)

    def multiply(k):
        wait(pt.at[origin(k, other), other, other], fwd_r.at[2 * (k - 1)])
        wait(pt.at[origin(k, other), other, c], fwd_r.at[2 * (k - 1) + 1])
        below, above = product(origin(k, 0), 0), product(origin(k, 1), 1)
        if k < 4:
            hts[:, :, 2 * k - 1] = below.reshape(NY, NX, 8, 512)
            hts[:, :, 2 * k] = above.reshape(NY, NX, 8, 512)
            ks[:, :, k - 1] = side_by_side(below, above)
        elif k == 4:
            both = below + above
            hts[:, :, 7] = both.reshape(NY, NX, 8, 512)
            own = hts[:, :, 0].reshape(128, 512)
            ks[:, :, 3] = 0.5 * side_by_side(own, both)
        else:
            d = 8 - k
            hts[:, :, 2 * d] = hts[:, :, 2 * d] + below.reshape(NY, NX, 8, 512)
            hts[:, :, 2 * d - 1] = hts[:, :, 2 * d - 1] + above.reshape(NY, NX, 8, 512)

    def share_early(part):
        slots = EARLY[part]
        kr[t, slots] = ks[ty, tx, slots]

        def to_peer(i):
            to = lax.rem(t + i, NT)
            send(
                ks.at[lax.div(to, NX), lax.rem(to, NX), slots], kr.at[t, slots],
                rs_s.at[part], rs_r.at[part], to, q,
            )

        each(1, 16, to_peer)

    def reduce_early(part):
        slots = EARLY[part]
        wait(kr.at[0:15, slots], rs_r.at[part])
        total = kr[0, slots]
        for source in range(1, NT):
            total = total + kr[source, slots]
        total = total * inverse_count
        for i in range(2):
            left, right = PAIRS[slots.start + i]
            dn[chunk_at(left)] = total[i]
            dn[chunk_at(right)] = pltpu.roll(total[i], WIDTH, 1)

    def first_phase(group):
        first, n = GROUPS[group]
        slots = slice(first, first + n)
        r1[0, tx, :, slots] = hts[:, tx, slots, :, 0:256]
        r1[1, ty, :, slots] = hts[ty, :, slots, :, 256:512]
        for i in range(1, 4):
            send(
                hts.at[:, lax.rem(tx + i, NX), slots, :, 0:256], r1.at[0, tx, :, slots],
                r1_s.at[2 * group], r1_r.at[2 * group], along_x(i), q,
            )
            send(
                hts.at[lax.rem(ty + i, NY), :, slots, :, 256:512], r1.at[1, ty, :, slots],
                r1_s.at[2 * group + 1], r1_r.at[2 * group + 1], along_y(i), q,
            )

    def second_phase(group):
        first, n = GROUPS[group]
        slots = slice(first, first + n)
        for part in range(2):
            wait(r1.at[part, 0:3, :, slots], r1_r.at[2 * group + part])
            p1[part, :, slots] = (
                (r1[part, 0, :, slots] + r1[part, 1, :, slots])
                + (r1[part, 2, :, slots] + r1[part, 3, :, slots])
            )
            me, size = (ty, NY) if part == 0 else (tx, NX)
            r2[part, me, slots] = p1[part, me, slots]
            for i in range(1, 4):
                send(
                    p1.at[part, lax.rem(me + i, size), slots], r2.at[part, me, slots],
                    r2_s.at[2 * group + part], r2_r.at[2 * group + part],
                    along_y(i) if part == 0 else along_x(i), q,
                )

    def reduce_group(group):
        first, n = GROUPS[group]
        slots = slice(first, first + n)
        for part in range(2):
            wait(r2.at[part, 0:3, slots], r2_r.at[2 * group + part])
            total = (r2[part, 0, slots] + r2[part, 1, slots]) + (r2[part, 2, slots] + r2[part, 3, slots])
            red[slots, :, 256 * part:256 * (part + 1)] = total * inverse_count

    def gather_first(batch):
        slots = BATCHES[batch]
        hta[slots, ty, tx] = red[slots]
        for i in range(1, 4):
            ref = hta.at[slots, ty, tx, :, 0:256]
            send(ref, ref, ha_s.at[4 * batch], ha_r.at[4 * batch], along_x(i), q)
            ref = hta.at[slots, ty, tx, :, 256:512]
            send(ref, ref, ha_s.at[4 * batch + 1], ha_r.at[4 * batch + 1], along_y(i), q)

    def gather_second(batch):
        slots = BATCHES[batch]
        wait(hta.at[slots, 0, 0:3, :, 0:256], ha_r.at[4 * batch])
        wait(hta.at[slots, 0, 0:3, :, 256:512], ha_r.at[4 * batch + 1])
        for i in range(1, 4):
            ref = hta.at[slots, ty, :, :, 0:256]
            send(ref, ref, ha_s.at[4 * batch + 2], ha_r.at[4 * batch + 2], along_y(i), q)
            ref = hta.at[slots, :, tx, :, 256:512]
            send(ref, ref, ha_s.at[4 * batch + 3], ha_r.at[4 * batch + 3], along_x(i), q)

    def gather_end(batch):
        slots = BATCHES[batch]
        wait(hta.at[slots, 0:3, :, :, 0:256], ha_r.at[4 * batch + 2])
        wait(hta.at[slots, 0:3, :, :, 256:512], ha_r.at[4 * batch + 3])
        for slot in range(slots.start, slots.stop):
            rows = pl.ds(pl.multiple_of(128 * chunk_at(slot), 128), 128)
            block = hta[slot].reshape(128, 512)
            high = block.astype(BF)
            hh[rows, :] = high
            hl[rows, :] = (block - high.astype(F32)).astype(BF)

    own = product(z, 0) + product(z, 1)
    hts[:, :, 0] = own.reshape(NY, NX, 8, 512)
    first_phase(0)
    pass_on(1)
    multiply(1)
    pass_on(2)
    multiply(2)
    share_early(0)
    second_phase(0)
    pass_on(3)
    multiply(3)
    reduce_group(0)
    pass_on(4)
    multiply(4)
    share_early(1)
    first_phase(1)
    reduce_early(0)
    pass_on(5)
    multiply(5)
    first_phase(2)
    reduce_early(1)

    lanes = lax.broadcasted_iota(jnp.int32, (64, 128), 1)
    own = dn[...].reshape(64, 128)
    own = jnp.where(c == 0, own, pltpu.roll(own, 64, 1))
    own = jnp.where(lax.div(lanes, 64) == c, own, 0.0)
    dsend[0] = own[0:32].astype(BF)
    dsend[1] = own[32:64].astype(BF)
    send(dsend.at[other], drecv, dsib_s.at[0], dsib_r.at[0], t, sibling)
    pass_on(6)
    wait(drecv, dsib_r.at[0])
    here = (dsend[c].astype(F32) + drecv[...].astype(F32)).astype(BF).reshape(2, 16, 128)
    dzs[...] = here
    my_lanes = pl.ds(pl.multiple_of(z * 128, 128), 128)
    drho[ty, tx, c, :, :, my_lanes] = here

    def along_z(i):
        send(
            dzs, drho.at[ty, tx, c, :, :, my_lanes], dz_s.at[0], dz_r.at[0],
            t, 2 * lax.rem(z + i, NZ) + c,
        )

    each(1, NZ, along_z)

    multiply(6)
    first_phase(3)
    second_phase(1)
    pass_on(7)
    second_phase(2)
    multiply(7)
    first_phase(4)

    wait(drho.at[ty, tx, c, :, :, 0:896], dz_r.at[0])

    for i in range(1, 4):
        ref = drho.at[ty, tx, c, 0]
        send(ref, ref, dxy_s.at[0], dxy_r.at[0], along_x(i), q)
        ref = drho.at[ty, tx, c, 1]
        send(ref, ref, dxy_s.at[1], dxy_r.at[1], along_y(i), q)
    reduce_group(1)
    reduce_group(2)
    gather_first(0)
    second_phase(3)
    wait(drho.at[0, 0:3, c, 0], dxy_r.at[0])
    for i in range(1, 4):
        ref = drho.at[ty, :, c, 0]
        send(ref, ref, dxy_s.at[2], dxy_r.at[2], along_y(i), q)
    wait(drho.at[0, 0:3, c, 1], dxy_r.at[1])
    for i in range(1, 4):
        ref = drho.at[:, tx, c, 1]
        send(ref, ref, dxy_s.at[3], dxy_r.at[3], along_x(i), q)
    ref = drho.at[ty, :, c, 0]
    send(ref, ref, df_s.at[0], df_r.at[0], t, sibling)
    ref = drho.at[:, tx, c, 1]
    send(ref, ref, df_s.at[1], df_r.at[1], t, sibling)

    def share_pruned(i):
        to = lax.rem(q + i, NQ)
        send(pts.at[lax.rem(to, 2)], pall.at[q], pz_s.at[0], pz_r.at[0], t, to)

    each(1, NQ, share_pruned)

    second_phase(4)
    reduce_group(3)
    gather_second(0)
    reduce_group(4)
    gather_first(1)
    wait(drho.at[0:3, :, c, 0], dxy_r.at[2])
    for i in range(1, 4):
        ref = drho.at[lax.rem(ty + i, NY), :, c, 0]
        send(ref, ref, df_s.at[2], df_r.at[2], t, sibling)
    wait(drho.at[0:3, :, c, 1], dxy_r.at[3])
    for i in range(1, 4):
        ref = drho.at[:, lax.rem(tx + i, NX), c, 1]
        send(ref, ref, df_s.at[3], df_r.at[3], t, sibling)
    gather_second(1)
    wait(drho.at[0, :, other, 0], df_r.at[0])
    wait(drho.at[0, :, other, 1], df_r.at[1])
    wait(drho.at[0:3, :, other, 0], df_r.at[2])
    wait(drho.at[0:3, :, other, 1], df_r.at[3])

    lane = lax.broadcasted_iota(jnp.int32, (8, 128), 1)
    row = lax.broadcasted_iota(jnp.int32, (8, 128), 0)
    diagonal = jnp.zeros((8, 128), F32)
    for i in range(NT):
        block = drho[i // NX, i % NX].reshape(64, 1024).astype(F32).reshape(8, 8, 1024)
        g[:, i] = block
        for zo in range(NZ):
            diagonal = diagonal + jnp.where(
                lane == 8 * i + row, block[zo][:, 128 * zo:128 * (zo + 1)], 0.0
            )
    trace = 2.0 * jnp.sum(diagonal, axis=(0, 1), keepdims=True)
    damping = trace * (0.01 / B)
    wide_row = lax.broadcasted_iota(jnp.int32, (256, 256), 0)
    wide_lane = lax.broadcasted_iota(jnp.int32, (256, 256), 1)
    squares = jnp.zeros((1, 256), F32)
    for i in range(4):
        for j in range(i, 4):
            upper = g[2 * i:2 * i + 2, :, :, 256 * j:256 * (j + 1)].reshape(256, 256)
            lower = g[2 * j:2 * j + 2, :, :, 256 * i:256 * (i + 1)].reshape(256, 256)
            block = upper + lower.T
            total = jnp.sum(block * block, axis=0, keepdims=True)
            squares = squares + (total if i == j else 2.0 * total)
            if i == j:
                block = block + jnp.where(wide_row == wide_lane, damping, 0.0)
            g[2 * i:2 * i + 2, :, :, 256 * j:256 * (j + 1)] = block.reshape(2, 16, 8, 256)
            gb[0, 256 * i:256 * (i + 1), 256 * j:256 * (j + 1)] = block.astype(BF)
            if i != j:
                gb[0, 256 * j:256 * (j + 1), 256 * i:256 * (i + 1)] = block.T.astype(BF)
    norm = jnp.sum(squares, axis=(0, 1), keepdims=True) + damping * (2.0 * trace + B * damping)
    scale = 1.0 / jnp.sqrt(norm)

    for k in range(ITERS - 1):
        for i in range(4):
            n = 1024 - 256 * i
            product = dot(gb[k, 256 * i:256 * (i + 1), :], gb[k, :, 256 * i:1024])
            old = g[2 * i:2 * i + 2, :, :, 256 * i:1024].reshape(256, n)
            if k == 0:
                new = (2.0 * scale) * old - (scale * scale) * product
            else:
                new = 2.0 * old - product
            if k < ITERS - 2:
                g[2 * i:2 * i + 2, :, :, 256 * i:1024] = new.reshape(2, 16, 8, n)
            gb[k + 1, 256 * i:256 * (i + 1), 256 * i:1024] = new.astype(BF)
            for j in range(i + 1, 4):
                mirrored = new[:, 256 * (j - i):256 * (j - i + 1)].T
                gb[k + 1, 256 * j:256 * (j + 1), 256 * i:256 * (i + 1)] = mirrored.astype(BF)

    wait(pall.at[0:15], pz_r.at[0])
    for i in range(8):
        piece = pall[2 * i:2 * i + 2].reshape(128, 256).astype(F32).T
        y[:, 128 * i:128 * (i + 1)] = piece
        yb[0, 0:256, 128 * i:128 * (i + 1)] = piece.astype(BF)

    for k in range(ITERS):
        for i in range(4):
            columns = slice(256 * i, 256 * (i + 1))
            if k == 0:
                step = scale * dot(yb[0, 0:256], gb[0, :, columns])
            else:
                both = dot(yb[k % 2], gb[k, :, columns])
                step = both[0:256] + both[256:512]
            new = 2.0 * y[:, columns] - step
            if k == ITERS - 1:
                new = new * scale
            high = new.astype(BF)
            low = (new - high.astype(F32)).astype(BF)
            if k < ITERS - 1:
                y[:, columns] = new
                yb[(k + 1) % 2, 0:256, columns] = high
                yb[(k + 1) % 2, 256:512, columns] = low
            else:
                yx[c, 0:256, columns] = high
                yx[c, 256:512, columns] = low

    send(yx.at[c], yx.at[c], yx_s.at[0], yx_r.at[0], t, sibling)

    gather_end(0)
    gather_end(1)

    def finish(part):
        rows = pl.ds(pl.multiple_of(part * 256, 256), 256)
        both = dot(yx[part], hh[...])
        correction = both[0:256] + both[256:512] + dot(yx[part, 0:256], hl[...])
        kept = m[rows, :].astype(F32)
        out_ref[rows, :] = (kept * (w[rows, :].astype(F32) - correction)).astype(BF)

    finish(c)
    wait(yx.at[other], yx_r.at[0])
    finish(other)

    wait(pt.at[z, other, c], sib_s.at[0])
    wait(pt.at[z, c, c], sib_s.at[1])
    for at in range(28):
        wait(pt.at[z, c, c, 0:32], ring_s.at[at])
    for at in range(14):
        wait(pt.at[z, c, c], fwd_s.at[at])
    for group in range(5):
        first, n = GROUPS[group]
        for part in range(2):
            wait(r1.at[part, 0:3, :, first:first + n], r1_s.at[2 * group + part])
            wait(r2.at[part, 0:3, first:first + n], r2_s.at[2 * group + part])
    for part in range(2):
        wait(kr.at[0:15, EARLY[part]], rs_s.at[part])
    wait(dsend.at[other], dsib_s.at[0])
    wait(drho.at[ty, tx, c, :, :, 0:896], dz_s.at[0])
    wait(pall.at[0:15], pz_s.at[0])
    wait(drho.at[0, 0:3, c, 0], dxy_s.at[0])
    wait(drho.at[0, 0:3, c, 1], dxy_s.at[1])
    wait(drho.at[0:3, :, c, 0], dxy_s.at[2])
    wait(drho.at[0:3, :, c, 1], dxy_s.at[3])
    wait(drho.at[0, :, c, 0], df_s.at[0])
    wait(drho.at[0, :, c, 1], df_s.at[1])
    wait(drho.at[0:3, :, c, 0], df_s.at[2])
    wait(drho.at[0:3, :, c, 1], df_s.at[3])
    for batch in range(2):
        slots = BATCHES[batch]
        wait(hta.at[slots, 0, 0:3, :, 0:256], ha_s.at[4 * batch])
        wait(hta.at[slots, 0, 0:3, :, 256:512], ha_s.at[4 * batch + 1])
        wait(hta.at[slots, 0:3, :, :, 0:256], ha_s.at[4 * batch + 2])
        wait(hta.at[slots, 0:3, :, :, 256:512], ha_s.at[4 * batch + 3])
    wait(yx.at[c], yx_s.at[0])


def per_device(activations, weight, keep_mask):
    sems = (4, 2, 2, 28, 28, 14, 14, 2, 2, 10, 10, 10, 10, 1, 1, 1, 1, 4, 4, 4, 4, 1, 1, 8, 8, 1, 1)
    return pl.pallas_call(
        kernel,
        out_shape=jax.ShapeDtypeStruct(weight.shape, BF),
        in_specs=[pl.BlockSpec(memory_space=pl.ANY)] * 3,
        out_specs=pl.BlockSpec(memory_space=pltpu.VMEM),
        scratch_shapes=[
            pltpu.VMEM((2048, 512), BF),
            pltpu.VMEM((512, 512), BF),
            pltpu.VMEM((512, 512), jnp.int32),
            pltpu.VMEM((NZ, 2, 2, WIDTH, 1024), BF),
            pltpu.VMEM((NY, NX, 8, 8, 512), F32),
            pltpu.VMEM((NY, NX, 4, 8, 128), F32),
            pltpu.VMEM((NT, 4, 8, 128), F32),
            pltpu.VMEM((2, 4, 4, 8, 8, 256), F32),
            pltpu.VMEM((2, 4, 8, 8, 256), F32),
            pltpu.VMEM((2, 4, 8, 8, 256), F32),
            pltpu.VMEM((8, 8, 512), F32),
            pltpu.VMEM((NZ, 8, 128), F32),
            pltpu.VMEM((2, 32, 128), BF),
            pltpu.VMEM((32, 128), BF),
            pltpu.VMEM((2, 16, 128), BF),
            pltpu.VMEM((NY, NX, 2, 2, 16, 1024), BF),
            pltpu.VMEM((NZ, NT, 8, 1024), F32),
            pltpu.VMEM((ITERS, 1024, 1024), BF),
            pltpu.VMEM((NZ, NY, NX, 8, 512), F32),
            pltpu.VMEM((1024, 512), BF),
            pltpu.VMEM((1024, 512), BF),
            pltpu.VMEM((2, WIDTH, 256), BF),
            pltpu.VMEM((NQ, WIDTH, 256), BF),
            pltpu.VMEM((256, 1024), F32),
            pltpu.VMEM((2, 512, 1024), BF),
            pltpu.VMEM((2, 512, 1024), BF),
        ] + [pltpu.SemaphoreType.DMA((n,)) for n in sems],
        compiler_params=pltpu.CompilerParams(
            collective_id=0, has_side_effects=True, vmem_limit_bytes=56 << 20
        ),
    )(activations, weight, keep_mask)


def solution(mesh):
    return jax.shard_map(
        per_device,
        mesh=mesh,
        in_specs=(P("tok", "col"), P("tok", "col"), P("tok", "col")),
        out_specs=P("tok", "col"),
        check_vma=False,
    )
```

```python
import functools

import jax
import jax.numpy as jnp
from jax import lax
from jax.experimental import pallas as pl
from jax.experimental.pallas import tpu as pltpu
from jax.sharding import PartitionSpec as P

B = 1024
ITERS = 4
NZ, NY, NX, NT, NQ = 8, 4, 4, 16, 16
WIDTH = 64
OFFSETS = (0, -1, 1, -2, 2, -3, 3, 4)
GROUPS = ((0, 1), (7, 1), (5, 2), (3, 2), (1, 2))
EARLY = (slice(0, 2), slice(2, 4))
PAIRS = ((1, 2), (3, 4), (5, 6), (0, 7))
BATCHES = (slice(5, 8), slice(0, 5))
BF, F32 = jnp.bfloat16, jnp.float32


def dot(a, b):
    return jnp.dot(a, b, preferred_element_type=F32)


def kernel(
    a_hbm, w_hbm, m_hbm, out_ref,
    a, w, m, pt, hts, ks, kr, r1, p1, r2, red, dn, dsend, drecv, dzs, drho, g, gb, hta, hh, hl, pts, pall, y, yb, yx,
    load_sem, sib_s, sib_r, ring_s, ring_r, fwd_s, fwd_r, rs_s, rs_r, r1_s, r1_r, r2_s, r2_r, dsib_s, dsib_r, dz_s, dz_r,
    dxy_s, dxy_r, df_s, df_r, pz_s, pz_r, ha_s, ha_r, yx_s, yx_r,
):
    t, q = lax.axis_index("tok"), lax.axis_index("col")
    ty, tx = lax.div(t, NX), lax.rem(t, NX)
    z, c = lax.div(q, 2), lax.rem(q, 2)
    other = 1 - c
    sibling = 2 * z + other
    inverse_count = 1.0 / (a.shape[0] * NT)

    def send(src, dst, send_sem, recv_sem, tok, col):
        pltpu.make_async_remote_copy(
            src_ref=src, dst_ref=dst, send_sem=send_sem, recv_sem=recv_sem,
            device_id=(tok, col), device_id_type=pl.DeviceIdType.MESH,
        ).start()

    def wait(ref, sem):
        pltpu.make_async_copy(ref, ref, sem).wait()

    def each(first, last, body):
        def step(i, carry):
            body(i)
            return carry
        lax.fori_loop(first, last, step, 0)

    loads = [
        pltpu.make_async_copy(a_hbm.at[:, 0:128], a.at[:, 0:128], load_sem.at[0]),
        pltpu.make_async_copy(a_hbm.at[:, 128:512], a.at[:, 128:512], load_sem.at[1]),
        pltpu.make_async_copy(w_hbm, w, load_sem.at[2]),
        pltpu.make_async_copy(m_hbm, m, load_sem.at[3]),
    ]
    for load in loads:
        load.start()

    barrier = pltpu.get_barrier_semaphore()

    def greet(i):
        pl.semaphore_signal(
            barrier, inc=1, device_id=(lax.rem(t + i, NT), q), device_id_type=pl.DeviceIdType.MESH
        )
        pl.semaphore_signal(
            barrier, inc=1, device_id=(t, lax.rem(q + i, NQ)), device_id_type=pl.DeviceIdType.MESH
        )

    each(1, 16, greet)

    loads[0].wait()
    for half in range(2):
        for part in range(2):
            rows = half * 1024 + part * 512
            piece = a[rows:rows + 512, 0:128].astype(F32).T
            pt[z, half, c, :, part * 512:(part + 1) * 512] = piece[0:WIDTH].astype(BF)
    pl.semaphore_wait(barrier, 30)

    following = lax.rem(z + NZ + 1 - 2 * c, NZ)

    def origin(k, core):
        return lax.rem(z + NZ + (2 * core - 1) * k, NZ)

    def ring(k, v):
        u = c if v < 4 else other
        ref = pt.at[origin(k - 1, c), c, u, 16 * (v % 4):16 * (v % 4) + 16]
        at = 8 * (k - 1) + v
        send(ref, ref, ring_s.at[at], ring_r.at[at], t, 2 * following + c)

    send(pt.at[z, other, c], pt.at[z, other, c], sib_s.at[0], sib_r.at[0], t, sibling)
    for v in range(4):
        ring(1, v)
    send(pt.at[z, c, c], pt.at[z, c, c], sib_s.at[1], sib_r.at[1], t, sibling)
    wait(pt.at[z, c, other], sib_r.at[0])
    for v in range(4, 8):
        ring(1, v)

    loads[2].wait()
    loads[3].wait()
    pruned = jnp.where(m[:, 0:128] == 0, w[:, 0:128].astype(F32), 0.0).T
    pts[0] = pruned[0:WIDTH, 0:256].astype(BF)
    pts[1] = pruned[0:WIDTH, 256:512].astype(BF)
    pall[q] = pts[c]

    loads[1].wait()
    wait(pt.at[z, other, other], sib_r.at[1])

    def along_x(i):
        return NX * ty + lax.rem(tx + i, NX)

    def along_y(i):
        return NX * lax.rem(ty + i, NY) + tx

    def chunk_at(slot):
        return lax.rem(z + OFFSETS[slot] + NZ, NZ)

    def product(chunk, half):
        rows = pt[chunk, half].reshape(128, 1024)
        return dot(rows, a[1024 * half:1024 * (half + 1), :])

    def pass_on(k):
        for v in range(8):
            u = c if v < 4 else other
            wait(
                pt.at[origin(k, c), c, u, 16 * (v % 4):16 * (v % 4) + 16], ring_r.at[8 * (k - 1) + v]
            )
            if k < 7:
                ring(k + 1, v)
            if v % 4 == 3:
                ref = pt.at[origin(k, c), c, u]
                at = 2 * (k - 1) + v // 4
                send(ref, ref, fwd_s.at[at], fwd_r.at[at], t, sibling)

    def side_by_side(left, right):
        lanes = lax.broadcasted_iota(jnp.int32, (128, 128), 1)
        packed = jnp.where(lanes < WIDTH, left[:, 0:128], pltpu.roll(right[:, 0:128], WIDTH, 1))
        return packed.reshape(NY, NX, 8, 128)

    def multiply(k):
        wait(pt.at[origin(k, other), other, other], fwd_r.at[2 * (k - 1)])
        wait(pt.at[origin(k, other), other, c], fwd_r.at[2 * (k - 1) + 1])
        below, above = product(origin(k, 0), 0), product(origin(k, 1), 1)
        if k < 4:
            hts[:, :, 2 * k - 1] = below.reshape(NY, NX, 8, 512)
            hts[:, :, 2 * k] = above.reshape(NY, NX, 8, 512)
            ks[:, :, k - 1] = side_by_side(below, above)
        elif k == 4:
            both = below + above
            hts[:, :, 7] = both.reshape(NY, NX, 8, 512)
            own = hts[:, :, 0].reshape(128, 512)
            ks[:, :, 3] = 0.5 * side_by_side(own, both)
        else:
            d = 8 - k
            hts[:, :, 2 * d] = hts[:, :, 2 * d] + below.reshape(NY, NX, 8, 512)
            hts[:, :, 2 * d - 1] = hts[:, :, 2 * d - 1] + above.reshape(NY, NX, 8, 512)

    def share_early(part):
        slots = EARLY[part]
        kr[t, slots] = ks[ty, tx, slots]

        def to_peer(i):
            to = lax.rem(t + i, NT)
            send(
                ks.at[lax.div(to, NX), lax.rem(to, NX), slots], kr.at[t, slots],
                rs_s.at[part], rs_r.at[part], to, q,
            )

        each(1, 16, to_peer)

    def reduce_early(part):
        slots = EARLY[part]
        wait(kr.at[0:15, slots], rs_r.at[part])
        total = kr[0, slots]
        for source in range(1, NT):
            total = total + kr[source, slots]
        total = total * inverse_count
        for i in range(2):
            left, right = PAIRS[slots.start + i]
            dn[chunk_at(left)] = total[i]
            dn[chunk_at(right)] = pltpu.roll(total[i], WIDTH, 1)

    def first_phase(group):
        first, n = GROUPS[group]
        slots = slice(first, first + n)
        r1[0, tx, :, slots] = hts[:, tx, slots, :, 0:256]
        r1[1, ty, :, slots] = hts[ty, :, slots, :, 256:512]
        for i in range(1, 4):
            send(
                hts.at[:, lax.rem(tx + i, NX), slots, :, 0:256], r1.at[0, tx, :, slots],
                r1_s.at[2 * group], r1_r.at[2 * group], along_x(i), q,
            )
            send(
                hts.at[lax.rem(ty + i, NY), :, slots, :, 256:512], r1.at[1, ty, :, slots],
                r1_s.at[2 * group + 1], r1_r.at[2 * group + 1], along_y(i), q,
            )

    def second_phase(group):
        first, n = GROUPS[group]
        slots = slice(first, first + n)
        for part in range(2):
            wait(r1.at[part, 0:3, :, slots], r1_r.at[2 * group + part])
            p1[part, :, slots] = (
                (r1[part, 0, :, slots] + r1[part, 1, :, slots])
                + (r1[part, 2, :, slots] + r1[part, 3, :, slots])
            )
            me, size = (ty, NY) if part == 0 else (tx, NX)
            r2[part, me, slots] = p1[part, me, slots]
            for i in range(1, 4):
                send(
                    p1.at[part, lax.rem(me + i, size), slots], r2.at[part, me, slots],
                    r2_s.at[2 * group + part], r2_r.at[2 * group + part],
                    along_y(i) if part == 0 else along_x(i), q,
                )

    def reduce_group(group):
        first, n = GROUPS[group]
        slots = slice(first, first + n)
        for part in range(2):
            wait(r2.at[part, 0:3, slots], r2_r.at[2 * group + part])
            total = (r2[part, 0, slots] + r2[part, 1, slots]) + (r2[part, 2, slots] + r2[part, 3, slots])
            red[slots, :, 256 * part:256 * (part + 1)] = total * inverse_count

    def gather_first(batch):
        slots = BATCHES[batch]
        hta[slots, ty, tx] = red[slots]
        for i in range(1, 4):
            ref = hta.at[slots, ty, tx, :, 0:256]
            send(ref, ref, ha_s.at[4 * batch], ha_r.at[4 * batch], along_x(i), q)
            ref = hta.at[slots, ty, tx, :, 256:512]
            send(ref, ref, ha_s.at[4 * batch + 1], ha_r.at[4 * batch + 1], along_y(i), q)

    def gather_second(batch):
        slots = BATCHES[batch]
        wait(hta.at[slots, 0, 0:3, :, 0:256], ha_r.at[4 * batch])
        wait(hta.at[slots, 0, 0:3, :, 256:512], ha_r.at[4 * batch + 1])
        for i in range(1, 4):
            ref = hta.at[slots, ty, :, :, 0:256]
            send(ref, ref, ha_s.at[4 * batch + 2], ha_r.at[4 * batch + 2], along_y(i), q)
            ref = hta.at[slots, :, tx, :, 256:512]
            send(ref, ref, ha_s.at[4 * batch + 3], ha_r.at[4 * batch + 3], along_x(i), q)

    def gather_end(batch):
        slots = BATCHES[batch]
        wait(hta.at[slots, 0:3, :, :, 0:256], ha_r.at[4 * batch + 2])
        wait(hta.at[slots, 0:3, :, :, 256:512], ha_r.at[4 * batch + 3])
        for slot in range(slots.start, slots.stop):
            rows = pl.ds(pl.multiple_of(128 * chunk_at(slot), 128), 128)
            block = hta[slot].reshape(128, 512)
            high = block.astype(BF)
            hh[rows, :] = high
            hl[rows, :] = (block - high.astype(F32)).astype(BF)

    own = product(z, 0) + product(z, 1)
    hts[:, :, 0] = own.reshape(NY, NX, 8, 512)
    first_phase(0)
    pass_on(1)
    multiply(1)
    pass_on(2)
    multiply(2)
    share_early(0)
    second_phase(0)
    pass_on(3)
    multiply(3)
    reduce_group(0)
    pass_on(4)
    multiply(4)
    share_early(1)
    first_phase(1)
    reduce_early(0)
    pass_on(5)
    multiply(5)
    first_phase(2)
    reduce_early(1)

    lanes = lax.broadcasted_iota(jnp.int32, (64, 128), 1)
    own = dn[...].reshape(64, 128)
    own = jnp.where(c == 0, own, pltpu.roll(own, 64, 1))
    own = jnp.where(lax.div(lanes, 64) == c, own, 0.0)
    dsend[0] = own[0:32].astype(BF)
    dsend[1] = own[32:64].astype(BF)
    send(dsend.at[other], drecv, dsib_s.at[0], dsib_r.at[0], t, sibling)
    pass_on(6)
    wait(drecv, dsib_r.at[0])
    here = (dsend[c].astype(F32) + drecv[...].astype(F32)).astype(BF).reshape(2, 16, 128)
    dzs[...] = here
    my_lanes = pl.ds(pl.multiple_of(z * 128, 128), 128)
    drho[ty, tx, c, :, :, my_lanes] = here

    def along_z(i):
        send(
            dzs, drho.at[ty, tx, c, :, :, my_lanes], dz_s.at[0], dz_r.at[0],
            t, 2 * lax.rem(z + i, NZ) + c,
        )

    each(1, NZ, along_z)

    multiply(6)
    first_phase(3)
    second_phase(1)
    pass_on(7)
    second_phase(2)
    multiply(7)
    first_phase(4)

    wait(drho.at[ty, tx, c, :, :, 0:896], dz_r.at[0])

    for i in range(1, 4):
        ref = drho.at[ty, tx, c, 0]
        send(ref, ref, dxy_s.at[0], dxy_r.at[0], along_x(i), q)
        ref = drho.at[ty, tx, c, 1]
        send(ref, ref, dxy_s.at[1], dxy_r.at[1], along_y(i), q)
    reduce_group(1)
    reduce_group(2)
    gather_first(0)
    second_phase(3)
    second_phase(4)
    wait(drho.at[0, 0:3, c, 0], dxy_r.at[0])
    for i in range(1, 4):
        ref = drho.at[ty, :, c, 0]
        send(ref, ref, dxy_s.at[2], dxy_r.at[2], along_y(i), q)
    wait(drho.at[0, 0:3, c, 1], dxy_r.at[1])
    for i in range(1, 4):
        ref = drho.at[:, tx, c, 1]
        send(ref, ref, dxy_s.at[3], dxy_r.at[3], along_x(i), q)
    ref = drho.at[ty, :, c, 0]
    send(ref, ref, df_s.at[0], df_r.at[0], t, sibling)
    ref = drho.at[:, tx, c, 1]
    send(ref, ref, df_s.at[1], df_r.at[1], t, sibling)

    def share_pruned(i):
        to = lax.rem(q + i, NQ)
        send(pts.at[lax.rem(to, 2)], pall.at[q], pz_s.at[0], pz_r.at[0], t, to)

    each(1, NQ, share_pruned)

    reduce_group(3)
    reduce_group(4)
    gather_first(1)
    wait(drho.at[0:3, :, c, 0], dxy_r.at[2])
    for i in range(1, 4):
        ref = drho.at[lax.rem(ty + i, NY), :, c, 0]
        send(ref, ref, df_s.at[2], df_r.at[2], t, sibling)
    wait(drho.at[0:3, :, c, 1], dxy_r.at[3])
    for i in range(1, 4):
        ref = drho.at[:, lax.rem(tx + i, NX), c, 1]
        send(ref, ref, df_s.at[3], df_r.at[3], t, sibling)
    gather_second(0)
    gather_second(1)
    wait(drho.at[0, :, other, 0], df_r.at[0])
    wait(drho.at[0, :, other, 1], df_r.at[1])
    wait(drho.at[0:3, :, other, 0], df_r.at[2])
    wait(drho.at[0:3, :, other, 1], df_r.at[3])

    lane = lax.broadcasted_iota(jnp.int32, (8, 128), 1)
    row = lax.broadcasted_iota(jnp.int32, (8, 128), 0)
    diagonal = jnp.zeros((8, 128), F32)
    for i in range(NT):
        block = drho[i // NX, i % NX].reshape(64, 1024).astype(F32).reshape(8, 8, 1024)
        g[:, i] = block
        for zo in range(NZ):
            diagonal = diagonal + jnp.where(
                lane == 8 * i + row, block[zo][:, 128 * zo:128 * (zo + 1)], 0.0
            )
    trace = 2.0 * jnp.sum(diagonal, axis=(0, 1), keepdims=True)
    damping = trace * (0.01 / B)
    wide_row = lax.broadcasted_iota(jnp.int32, (256, 256), 0)
    wide_lane = lax.broadcasted_iota(jnp.int32, (256, 256), 1)
    squares = jnp.zeros((1, 256), F32)
    for i in range(4):
        for j in range(i, 4):
            upper = g[2 * i:2 * i + 2, :, :, 256 * j:256 * (j + 1)].reshape(256, 256)
            lower = g[2 * j:2 * j + 2, :, :, 256 * i:256 * (i + 1)].reshape(256, 256)
            block = upper + lower.T
            total = jnp.sum(block * block, axis=0, keepdims=True)
            squares = squares + (total if i == j else 2.0 * total)
            if i == j:
                block = block + jnp.where(wide_row == wide_lane, damping, 0.0)
            g[2 * i:2 * i + 2, :, :, 256 * j:256 * (j + 1)] = block.reshape(2, 16, 8, 256)
            gb[0, 256 * i:256 * (i + 1), 256 * j:256 * (j + 1)] = block.astype(BF)
            if i != j:
                gb[0, 256 * j:256 * (j + 1), 256 * i:256 * (i + 1)] = block.T.astype(BF)
    norm = jnp.sum(squares, axis=(0, 1), keepdims=True) + damping * (2.0 * trace + B * damping)
    scale = 1.0 / jnp.sqrt(norm)

    for k in range(ITERS - 1):
        for i in range(4):
            n = 1024 - 256 * i
            product = dot(gb[k, 256 * i:256 * (i + 1), :], gb[k, :, 256 * i:1024])
            old = g[2 * i:2 * i + 2, :, :, 256 * i:1024].reshape(256, n)
            if k == 0:
                new = (2.0 * scale) * old - (scale * scale) * product
            else:
                new = 2.0 * old - product
            if k < ITERS - 2:
                g[2 * i:2 * i + 2, :, :, 256 * i:1024] = new.reshape(2, 16, 8, n)
            gb[k + 1, 256 * i:256 * (i + 1), 256 * i:1024] = new.astype(BF)
            for j in range(i + 1, 4):
                mirrored = new[:, 256 * (j - i):256 * (j - i + 1)].T
                gb[k + 1, 256 * j:256 * (j + 1), 256 * i:256 * (i + 1)] = mirrored.astype(BF)

    wait(pall.at[0:15], pz_r.at[0])
    for i in range(8):
        piece = pall[2 * i:2 * i + 2].reshape(128, 256).astype(F32).T
        y[:, 128 * i:128 * (i + 1)] = piece
        yb[0, 0:256, 128 * i:128 * (i + 1)] = piece.astype(BF)

    for k in range(ITERS):
        for i in range(4):
            columns = slice(256 * i, 256 * (i + 1))
            if k == 0:
                step = scale * dot(yb[0, 0:256], gb[0, :, columns])
            else:
                both = dot(yb[k % 2], gb[k, :, columns])
                step = both[0:256] + both[256:512]
            new = 2.0 * y[:, columns] - step
            if k == ITERS - 1:
                new = new * scale
            high = new.astype(BF)
            low = (new - high.astype(F32)).astype(BF)
            if k < ITERS - 1:
                y[:, columns] = new
                yb[(k + 1) % 2, 0:256, columns] = high
                yb[(k + 1) % 2, 256:512, columns] = low
            else:
                yx[c, 0:256, columns] = high
                yx[c, 256:512, columns] = low

    send(yx.at[c], yx.at[c], yx_s.at[0], yx_r.at[0], t, sibling)

    gather_end(0)
    gather_end(1)

    def finish(part):
        rows = pl.ds(pl.multiple_of(part * 256, 256), 256)
        both = dot(yx[part], hh[...])
        correction = both[0:256] + both[256:512] + dot(yx[part, 0:256], hl[...])
        kept = m[rows, :].astype(F32)
        out_ref[rows, :] = (kept * (w[rows, :].astype(F32) - correction)).astype(BF)

    finish(c)
    wait(yx.at[other], yx_r.at[0])
    finish(other)

    wait(pt.at[z, other, c], sib_s.at[0])
    wait(pt.at[z, c, c], sib_s.at[1])
    for at in range(56):
        wait(pt.at[z, c, c, 0:16], ring_s.at[at])
    for at in range(14):
        wait(pt.at[z, c, c], fwd_s.at[at])
    for group in range(5):
        first, n = GROUPS[group]
        for part in range(2):
            wait(r1.at[part, 0:3, :, first:first + n], r1_s.at[2 * group + part])
            wait(r2.at[part, 0:3, first:first + n], r2_s.at[2 * group + part])
    for part in range(2):
        wait(kr.at[0:15, EARLY[part]], rs_s.at[part])
    wait(dsend.at[other], dsib_s.at[0])
    wait(drho.at[ty, tx, c, :, :, 0:896], dz_s.at[0])
    wait(pall.at[0:15], pz_s.at[0])
    wait(drho.at[0, 0:3, c, 0], dxy_s.at[0])
    wait(drho.at[0, 0:3, c, 1], dxy_s.at[1])
    wait(drho.at[0:3, :, c, 0], dxy_s.at[2])
    wait(drho.at[0:3, :, c, 1], dxy_s.at[3])
    wait(drho.at[0, :, c, 0], df_s.at[0])
    wait(drho.at[0, :, c, 1], df_s.at[1])
    wait(drho.at[0:3, :, c, 0], df_s.at[2])
    wait(drho.at[0:3, :, c, 1], df_s.at[3])
    for batch in range(2):
        slots = BATCHES[batch]
        wait(hta.at[slots, 0, 0:3, :, 0:256], ha_s.at[4 * batch])
        wait(hta.at[slots, 0, 0:3, :, 256:512], ha_s.at[4 * batch + 1])
        wait(hta.at[slots, 0:3, :, :, 0:256], ha_s.at[4 * batch + 2])
        wait(hta.at[slots, 0:3, :, :, 256:512], ha_s.at[4 * batch + 3])
    wait(yx.at[c], yx_s.at[0])


def per_device(activations, weight, keep_mask):
    sems = (4, 2, 2, 56, 56, 14, 14, 2, 2, 10, 10, 10, 10, 1, 1, 1, 1, 4, 4, 4, 4, 1, 1, 8, 8, 1, 1)
    return pl.pallas_call(
        kernel,
        out_shape=jax.ShapeDtypeStruct(weight.shape, BF),
        in_specs=[pl.BlockSpec(memory_space=pl.ANY)] * 3,
        out_specs=pl.BlockSpec(memory_space=pltpu.VMEM),
        scratch_shapes=[
            pltpu.VMEM((2048, 512), BF),
            pltpu.VMEM((512, 512), BF),
            pltpu.VMEM((512, 512), jnp.int32),
            pltpu.VMEM((NZ, 2, 2, WIDTH, 1024), BF),
            pltpu.VMEM((NY, NX, 8, 8, 512), F32),
            pltpu.VMEM((NY, NX, 4, 8, 128), F32),
            pltpu.VMEM((NT, 4, 8, 128), F32),
            pltpu.VMEM((2, 4, 4, 8, 8, 256), F32),
            pltpu.VMEM((2, 4, 8, 8, 256), F32),
            pltpu.VMEM((2, 4, 8, 8, 256), F32),
            pltpu.VMEM((8, 8, 512), F32),
            pltpu.VMEM((NZ, 8, 128), F32),
            pltpu.VMEM((2, 32, 128), BF),
            pltpu.VMEM((32, 128), BF),
            pltpu.VMEM((2, 16, 128), BF),
            pltpu.VMEM((NY, NX, 2, 2, 16, 1024), BF),
            pltpu.VMEM((NZ, NT, 8, 1024), F32),
            pltpu.VMEM((ITERS, 1024, 1024), BF),
            pltpu.VMEM((NZ, NY, NX, 8, 512), F32),
            pltpu.VMEM((1024, 512), BF),
            pltpu.VMEM((1024, 512), BF),
            pltpu.VMEM((2, WIDTH, 256), BF),
            pltpu.VMEM((NQ, WIDTH, 256), BF),
            pltpu.VMEM((256, 1024), F32),
            pltpu.VMEM((2, 512, 1024), BF),
            pltpu.VMEM((2, 512, 1024), BF),
        ] + [pltpu.SemaphoreType.DMA((n,)) for n in sems],
        compiler_params=pltpu.CompilerParams(
            collective_id=0, has_side_effects=True, vmem_limit_bytes=56 << 20
        ),
    )(activations, weight, keep_mask)


def solution(mesh):
    return jax.shard_map(
        per_device,
        mesh=mesh,
        in_specs=(P("tok", "col"), P("tok", "col"), P("tok", "col")),
        out_specs=P("tok", "col"),
        check_vma=False,
    )
```

```python
import functools

import jax
import jax.numpy as jnp
from jax import lax
from jax.experimental import pallas as pl
from jax.experimental.pallas import tpu as pltpu
from jax.sharding import PartitionSpec as P

B = 1024
ITERS = 4
NZ, NY, NX, NT, NQ = 8, 4, 4, 16, 16
WIDTH = 64
OFFSETS = (0, -1, 1, -2, 2, -3, 3, 4)
GROUPS = ((0, 1), (7, 1), (5, 2), (3, 2), (1, 2))
EARLY = (slice(0, 2), slice(2, 4))
PAIRS = ((1, 2), (3, 4), (5, 6), (0, 7))
BATCHES = (slice(5, 8), slice(0, 5))
BF, F32 = jnp.bfloat16, jnp.float32


def dot(a, b):
    return jnp.dot(a, b, preferred_element_type=F32)


def kernel(
    a_hbm, w_hbm, m_hbm, out_ref,
    a, w, m, pt, hts, ks, kr, r1, p1, r2, red, dn, dsend, drecv, dzs, drho, g, gb, hta, hh, hl, pts, pall, y, yb, yx,
    load_sem, sib_s, sib_r, ring_s, ring_r, fwd_s, fwd_r, rs_s, rs_r, r1_s, r1_r, r2_s, r2_r, dsib_s, dsib_r, dz_s, dz_r,
    dxy_s, dxy_r, df_s, df_r, pz_s, pz_r, ha_s, ha_r, yx_s, yx_r,
):
    t, q = lax.axis_index("tok"), lax.axis_index("col")
    ty, tx = lax.div(t, NX), lax.rem(t, NX)
    z, c = lax.div(q, 2), lax.rem(q, 2)
    other = 1 - c
    sibling = 2 * z + other
    inverse_count = 1.0 / (a.shape[0] * NT)

    def send(src, dst, send_sem, recv_sem, tok, col):
        pltpu.make_async_remote_copy(
            src_ref=src, dst_ref=dst, send_sem=send_sem, recv_sem=recv_sem,
            device_id=(tok, col), device_id_type=pl.DeviceIdType.MESH,
        ).start()

    def wait(ref, sem):
        pltpu.make_async_copy(ref, ref, sem).wait()

    def each(first, last, body):
        def step(i, carry):
            body(i)
            return carry
        lax.fori_loop(first, last, step, 0)

    loads = [
        pltpu.make_async_copy(a_hbm.at[:, 0:128], a.at[:, 0:128], load_sem.at[0]),
        pltpu.make_async_copy(a_hbm.at[:, 128:512], a.at[:, 128:512], load_sem.at[1]),
        pltpu.make_async_copy(w_hbm, w, load_sem.at[2]),
        pltpu.make_async_copy(m_hbm, m, load_sem.at[3]),
    ]
    for load in loads:
        load.start()

    barrier = pltpu.get_barrier_semaphore()

    def greet(i):
        pl.semaphore_signal(
            barrier, inc=1, device_id=(lax.rem(t + i, NT), q), device_id_type=pl.DeviceIdType.MESH
        )
        pl.semaphore_signal(
            barrier, inc=1, device_id=(t, lax.rem(q + i, NQ)), device_id_type=pl.DeviceIdType.MESH
        )

    each(1, 16, greet)

    loads[0].wait()
    for half in range(2):
        for part in range(2):
            rows = half * 1024 + part * 512
            piece = a[rows:rows + 512, 0:128].astype(F32).T
            pt[z, half, c, :, part * 512:(part + 1) * 512] = piece[0:WIDTH].astype(BF)
    pl.semaphore_wait(barrier, 30)

    following = lax.rem(z + NZ + 1 - 2 * c, NZ)

    def origin(k, core):
        return lax.rem(z + NZ + (2 * core - 1) * k, NZ)

    def ring(k, v):
        u = c if v < 4 else other
        ref = pt.at[origin(k - 1, c), c, u, 16 * (v % 4):16 * (v % 4) + 16]
        at = 8 * (k - 1) + v
        send(ref, ref, ring_s.at[at], ring_r.at[at], t, 2 * following + c)

    send(pt.at[z, other, c], pt.at[z, other, c], sib_s.at[0], sib_r.at[0], t, sibling)
    for v in range(4):
        ring(1, v)
    send(pt.at[z, c, c], pt.at[z, c, c], sib_s.at[1], sib_r.at[1], t, sibling)
    wait(pt.at[z, c, other], sib_r.at[0])
    for v in range(4, 8):
        ring(1, v)

    loads[2].wait()
    loads[3].wait()
    pruned = jnp.where(m[:, 0:128] == 0, w[:, 0:128].astype(F32), 0.0).T
    pts[0] = pruned[0:WIDTH, 0:256].astype(BF)
    pts[1] = pruned[0:WIDTH, 256:512].astype(BF)
    pall[q] = pts[c]

    loads[1].wait()
    wait(pt.at[z, other, other], sib_r.at[1])

    def along_x(i):
        return NX * ty + lax.rem(tx + i, NX)

    def along_y(i):
        return NX * lax.rem(ty + i, NY) + tx

    def chunk_at(slot):
        return lax.rem(z + OFFSETS[slot] + NZ, NZ)

    def product(chunk, half):
        rows = pt[chunk, half].reshape(128, 1024)
        return dot(rows, a[1024 * half:1024 * (half + 1), :])

    def pass_on(k):
        for v in range(8):
            u = c if v < 4 else other
            wait(
                pt.at[origin(k, c), c, u, 16 * (v % 4):16 * (v % 4) + 16], ring_r.at[8 * (k - 1) + v]
            )
            if k < 7:
                ring(k + 1, v)
            if v % 4 == 3:
                ref = pt.at[origin(k, c), c, u]
                at = 2 * (k - 1) + v // 4
                send(ref, ref, fwd_s.at[at], fwd_r.at[at], t, sibling)

    def side_by_side(left, right):
        lanes = lax.broadcasted_iota(jnp.int32, (128, 128), 1)
        packed = jnp.where(lanes < WIDTH, left[:, 0:128], pltpu.roll(right[:, 0:128], WIDTH, 1))
        return packed.reshape(NY, NX, 8, 128)

    def multiply(k):
        wait(pt.at[origin(k, other), other, other], fwd_r.at[2 * (k - 1)])
        wait(pt.at[origin(k, other), other, c], fwd_r.at[2 * (k - 1) + 1])
        below, above = product(origin(k, 0), 0), product(origin(k, 1), 1)
        if k < 4:
            hts[:, :, 2 * k - 1] = below.reshape(NY, NX, 8, 512)
            hts[:, :, 2 * k] = above.reshape(NY, NX, 8, 512)
            ks[:, :, k - 1] = side_by_side(below, above)
        elif k == 4:
            both = below + above
            hts[:, :, 7] = both.reshape(NY, NX, 8, 512)
            own = hts[:, :, 0].reshape(128, 512)
            ks[:, :, 3] = 0.5 * side_by_side(own, both)
        else:
            d = 8 - k
            hts[:, :, 2 * d] = hts[:, :, 2 * d] + below.reshape(NY, NX, 8, 512)
            hts[:, :, 2 * d - 1] = hts[:, :, 2 * d - 1] + above.reshape(NY, NX, 8, 512)

    def share_early(part):
        slots = EARLY[part]
        kr[t, slots] = ks[ty, tx, slots]

        def to_peer(i):
            to = lax.rem(t + i, NT)
            send(
                ks.at[lax.div(to, NX), lax.rem(to, NX), slots], kr.at[t, slots],
                rs_s.at[part], rs_r.at[part], to, q,
            )

        each(1, 16, to_peer)

    def reduce_early(part):
        slots = EARLY[part]
        wait(kr.at[0:15, slots], rs_r.at[part])
        total = kr[0, slots]
        for source in range(1, NT):
            total = total + kr[source, slots]
        total = total * inverse_count
        for i in range(2):
            left, right = PAIRS[slots.start + i]
            dn[chunk_at(left)] = total[i]
            dn[chunk_at(right)] = pltpu.roll(total[i], WIDTH, 1)

    def first_phase(group):
        first, n = GROUPS[group]
        slots = slice(first, first + n)
        r1[0, tx, :, slots] = hts[:, tx, slots, :, 0:256]
        r1[1, ty, :, slots] = hts[ty, :, slots, :, 256:512]
        for i in range(1, 4):
            send(
                hts.at[:, lax.rem(tx + i, NX), slots, :, 0:256], r1.at[0, tx, :, slots],
                r1_s.at[2 * group], r1_r.at[2 * group], along_x(i), q,
            )
            send(
                hts.at[lax.rem(ty + i, NY), :, slots, :, 256:512], r1.at[1, ty, :, slots],
                r1_s.at[2 * group + 1], r1_r.at[2 * group + 1], along_y(i), q,
            )

    def second_phase(group):
        first, n = GROUPS[group]
        slots = slice(first, first + n)
        for part in range(2):
            wait(r1.at[part, 0:3, :, slots], r1_r.at[2 * group + part])
            p1[part, :, slots] = (
                (r1[part, 0, :, slots] + r1[part, 1, :, slots])
                + (r1[part, 2, :, slots] + r1[part, 3, :, slots])
            )
            me, size = (ty, NY) if part == 0 else (tx, NX)
            r2[part, me, slots] = p1[part, me, slots]
            for i in range(1, 4):
                send(
                    p1.at[part, lax.rem(me + i, size), slots], r2.at[part, me, slots],
                    r2_s.at[2 * group + part], r2_r.at[2 * group + part],
                    along_y(i) if part == 0 else along_x(i), q,
                )

    def reduce_group(group):
        first, n = GROUPS[group]
        slots = slice(first, first + n)
        for part in range(2):
            wait(r2.at[part, 0:3, slots], r2_r.at[2 * group + part])
            total = (r2[part, 0, slots] + r2[part, 1, slots]) + (r2[part, 2, slots] + r2[part, 3, slots])
            red[slots, :, 256 * part:256 * (part + 1)] = total * inverse_count

    def gather_first(batch):
        slots = BATCHES[batch]
        hta[slots, ty, tx] = red[slots]
        for i in range(1, 4):
            ref = hta.at[slots, ty, tx, :, 0:256]
            send(ref, ref, ha_s.at[4 * batch], ha_r.at[4 * batch], along_x(i), q)
            ref = hta.at[slots, ty, tx, :, 256:512]
            send(ref, ref, ha_s.at[4 * batch + 1], ha_r.at[4 * batch + 1], along_y(i), q)

    def gather_second(batch):
        slots = BATCHES[batch]
        wait(hta.at[slots, 0, 0:3, :, 0:256], ha_r.at[4 * batch])
        wait(hta.at[slots, 0, 0:3, :, 256:512], ha_r.at[4 * batch + 1])
        for i in range(1, 4):
            ref = hta.at[slots, ty, :, :, 0:256]
            send(ref, ref, ha_s.at[4 * batch + 2], ha_r.at[4 * batch + 2], along_y(i), q)
            ref = hta.at[slots, :, tx, :, 256:512]
            send(ref, ref, ha_s.at[4 * batch + 3], ha_r.at[4 * batch + 3], along_x(i), q)

    def gather_end(batch):
        slots = BATCHES[batch]
        wait(hta.at[slots, 0:3, :, :, 0:256], ha_r.at[4 * batch + 2])
        wait(hta.at[slots, 0:3, :, :, 256:512], ha_r.at[4 * batch + 3])
        for slot in range(slots.start, slots.stop):
            rows = pl.ds(pl.multiple_of(128 * chunk_at(slot), 128), 128)
            block = hta[slot].reshape(128, 512)
            high = block.astype(BF)
            hh[rows, :] = high
            hl[rows, :] = (block - high.astype(F32)).astype(BF)

    own = product(z, 0) + product(z, 1)
    hts[:, :, 0] = own.reshape(NY, NX, 8, 512)
    first_phase(0)
    pass_on(1)
    multiply(1)
    pass_on(2)
    multiply(2)
    share_early(0)
    second_phase(0)
    pass_on(3)
    multiply(3)
    reduce_group(0)
    pass_on(4)
    multiply(4)
    share_early(1)
    first_phase(1)
    reduce_early(0)
    pass_on(5)
    multiply(5)
    first_phase(2)
    reduce_early(1)

    lanes = lax.broadcasted_iota(jnp.int32, (64, 128), 1)
    own = dn[...].reshape(64, 128)
    own = jnp.where(c == 0, own, pltpu.roll(own, 64, 1))
    own = jnp.where(lax.div(lanes, 64) == c, own, 0.0)
    dsend[0] = own[0:32].astype(BF)
    dsend[1] = own[32:64].astype(BF)
    send(dsend.at[other], drecv, dsib_s.at[0], dsib_r.at[0], t, sibling)
    pass_on(6)
    wait(drecv, dsib_r.at[0])
    here = (dsend[c].astype(F32) + drecv[...].astype(F32)).astype(BF).reshape(2, 16, 128)
    dzs[...] = here
    my_lanes = pl.ds(pl.multiple_of(z * 128, 128), 128)
    drho[ty, tx, c, :, :, my_lanes] = here

    def along_z(i):
        send(
            dzs, drho.at[ty, tx, c, :, :, my_lanes], dz_s.at[0], dz_r.at[0],
            t, 2 * lax.rem(z + i, NZ) + c,
        )

    each(1, NZ, along_z)

    multiply(6)
    first_phase(3)
    second_phase(1)
    pass_on(7)
    second_phase(2)
    multiply(7)
    first_phase(4)

    wait(drho.at[ty, tx, c, :, :, 0:896], dz_r.at[0])

    for i in range(1, 4):
        ref = drho.at[ty, tx, c, 0]
        send(ref, ref, dxy_s.at[0], dxy_r.at[0], along_x(i), q)
        ref = drho.at[ty, tx, c, 1]
        send(ref, ref, dxy_s.at[1], dxy_r.at[1], along_y(i), q)
    reduce_group(1)
    reduce_group(2)
    gather_first(0)
    second_phase(3)
    second_phase(4)
    wait(drho.at[0, 0:3, c, 0], dxy_r.at[0])
    for i in range(1, 4):
        ref = drho.at[ty, :, c, 0]
        send(ref, ref, dxy_s.at[2], dxy_r.at[2], along_y(i), q)
    wait(drho.at[0, 0:3, c, 1], dxy_r.at[1])
    for i in range(1, 4):
        ref = drho.at[:, tx, c, 1]
        send(ref, ref, dxy_s.at[3], dxy_r.at[3], along_x(i), q)
    ref = drho.at[ty, :, c, 0]
    send(ref, ref, df_s.at[0], df_r.at[0], t, sibling)
    ref = drho.at[:, tx, c, 1]
    send(ref, ref, df_s.at[1], df_r.at[1], t, sibling)

    def share_pruned(i):
        to = lax.rem(q + i, NQ)
        send(pts.at[lax.rem(to, 2)], pall.at[q], pz_s.at[0], pz_r.at[0], t, to)

    each(1, NQ, share_pruned)

    reduce_group(3)
    reduce_group(4)
    gather_first(1)
    wait(drho.at[0:3, :, c, 0], dxy_r.at[2])
    for i in range(1, 4):
        ref = drho.at[lax.rem(ty + i, NY), :, c, 0]
        send(ref, ref, df_s.at[2], df_r.at[2], t, sibling)
    wait(drho.at[0:3, :, c, 1], dxy_r.at[3])
    for i in range(1, 4):
        ref = drho.at[:, lax.rem(tx + i, NX), c, 1]
        send(ref, ref, df_s.at[3], df_r.at[3], t, sibling)
    gather_second(0)
    gather_second(1)
    wait(drho.at[0, :, other, 0], df_r.at[0])
    wait(drho.at[0, :, other, 1], df_r.at[1])
    wait(drho.at[0:3, :, other, 0], df_r.at[2])
    wait(drho.at[0:3, :, other, 1], df_r.at[3])

    lane = lax.broadcasted_iota(jnp.int32, (8, 128), 1)
    row = lax.broadcasted_iota(jnp.int32, (8, 128), 0)
    diagonal = jnp.zeros((8, 128), F32)
    for i in range(NT):
        block = drho[i // NX, i % NX].reshape(64, 1024).astype(F32).reshape(8, 8, 1024)
        g[:, i] = block
        for zo in range(NZ):
            diagonal = diagonal + jnp.where(
                lane == 8 * i + row, block[zo][:, 128 * zo:128 * (zo + 1)], 0.0
            )
    trace = 2.0 * jnp.sum(diagonal, axis=(0, 1), keepdims=True)
    damping = trace * (0.01 / B)
    wide_row = lax.broadcasted_iota(jnp.int32, (256, 256), 0)
    wide_lane = lax.broadcasted_iota(jnp.int32, (256, 256), 1)
    squares = jnp.zeros((1, 256), F32)
    for i in range(4):
        for j in range(i, 4):
            upper = g[2 * i:2 * i + 2, :, :, 256 * j:256 * (j + 1)].reshape(256, 256)
            lower = g[2 * j:2 * j + 2, :, :, 256 * i:256 * (i + 1)].reshape(256, 256)
            block = upper + lower.T
            total = jnp.sum(block * block, axis=0, keepdims=True)
            squares = squares + (total if i == j else 2.0 * total)
            if i == j:
                block = block + jnp.where(wide_row == wide_lane, damping, 0.0)
            g[2 * i:2 * i + 2, :, :, 256 * j:256 * (j + 1)] = block.reshape(2, 16, 8, 256)
            gb[0, 256 * i:256 * (i + 1), 256 * j:256 * (j + 1)] = block.astype(BF)
            if i != j:
                gb[0, 256 * j:256 * (j + 1), 256 * i:256 * (i + 1)] = block.T.astype(BF)
    norm = jnp.sum(squares, axis=(0, 1), keepdims=True) + damping * (2.0 * trace + B * damping)
    scale = 1.0 / jnp.sqrt(norm)

    for k in range(ITERS - 1):
        for i in range(4):
            n = 1024 - 256 * i
            product = dot(gb[k, 256 * i:256 * (i + 1), :], gb[k, :, 256 * i:1024])
            old = g[2 * i:2 * i + 2, :, :, 256 * i:1024].reshape(256, n)
            if k == 0:
                new = (2.0 * scale) * old - (scale * scale) * product
            else:
                new = 2.0 * old - product
            if k < ITERS - 2:
                g[2 * i:2 * i + 2, :, :, 256 * i:1024] = new.reshape(2, 16, 8, n)
            gb[k + 1, 256 * i:256 * (i + 1), 256 * i:1024] = new.astype(BF)
            for j in range(i + 1, 4):
                mirrored = new[:, 256 * (j - i):256 * (j - i + 1)].T
                gb[k + 1, 256 * j:256 * (j + 1), 256 * i:256 * (i + 1)] = mirrored.astype(BF)

    wait(pall.at[0:15], pz_r.at[0])
    for i in range(8):
        piece = pall[2 * i:2 * i + 2].reshape(128, 256).astype(F32).T
        y[:, 128 * i:128 * (i + 1)] = piece
        yb[0, 0:256, 128 * i:128 * (i + 1)] = piece.astype(BF)

    for k in range(ITERS):
        if k == ITERS - 1:
            gather_end(0)
        for i in range(4):
            columns = slice(256 * i, 256 * (i + 1))
            if k == 0:
                step = scale * dot(yb[0, 0:256], gb[0, :, columns])
            else:
                both = dot(yb[k % 2], gb[k, :, columns])
                step = both[0:256] + both[256:512]
            new = 2.0 * y[:, columns] - step
            if k == ITERS - 1:
                new = new * scale
            high = new.astype(BF)
            low = (new - high.astype(F32)).astype(BF)
            if k < ITERS - 1:
                y[:, columns] = new
                yb[(k + 1) % 2, 0:256, columns] = high
                yb[(k + 1) % 2, 256:512, columns] = low
            else:
                yx[c, 0:256, columns] = high
                yx[c, 256:512, columns] = low

    send(yx.at[c], yx.at[c], yx_s.at[0], yx_r.at[0], t, sibling)

    gather_end(1)

    def finish(part):
        rows = pl.ds(pl.multiple_of(part * 256, 256), 256)
        both = dot(yx[part], hh[...])
        correction = both[0:256] + both[256:512] + dot(yx[part, 0:256], hl[...])
        kept = m[rows, :].astype(F32)
        out_ref[rows, :] = (kept * (w[rows, :].astype(F32) - correction)).astype(BF)

    finish(c)
    wait(yx.at[other], yx_r.at[0])
    finish(other)

    wait(pt.at[z, other, c], sib_s.at[0])
    wait(pt.at[z, c, c], sib_s.at[1])
    for at in range(56):
        wait(pt.at[z, c, c, 0:16], ring_s.at[at])
    for at in range(14):
        wait(pt.at[z, c, c], fwd_s.at[at])
    for group in range(5):
        first, n = GROUPS[group]
        for part in range(2):
            wait(r1.at[part, 0:3, :, first:first + n], r1_s.at[2 * group + part])
            wait(r2.at[part, 0:3, first:first + n], r2_s.at[2 * group + part])
    for part in range(2):
        wait(kr.at[0:15, EARLY[part]], rs_s.at[part])
    wait(dsend.at[other], dsib_s.at[0])
    wait(drho.at[ty, tx, c, :, :, 0:896], dz_s.at[0])
    wait(pall.at[0:15], pz_s.at[0])
    wait(drho.at[0, 0:3, c, 0], dxy_s.at[0])
    wait(drho.at[0, 0:3, c, 1], dxy_s.at[1])
    wait(drho.at[0:3, :, c, 0], dxy_s.at[2])
    wait(drho.at[0:3, :, c, 1], dxy_s.at[3])
    wait(drho.at[0, :, c, 0], df_s.at[0])
    wait(drho.at[0, :, c, 1], df_s.at[1])
    wait(drho.at[0:3, :, c, 0], df_s.at[2])
    wait(drho.at[0:3, :, c, 1], df_s.at[3])
    for batch in range(2):
        slots = BATCHES[batch]
        wait(hta.at[slots, 0, 0:3, :, 0:256], ha_s.at[4 * batch])
        wait(hta.at[slots, 0, 0:3, :, 256:512], ha_s.at[4 * batch + 1])
        wait(hta.at[slots, 0:3, :, :, 0:256], ha_s.at[4 * batch + 2])
        wait(hta.at[slots, 0:3, :, :, 256:512], ha_s.at[4 * batch + 3])
    wait(yx.at[c], yx_s.at[0])


def per_device(activations, weight, keep_mask):
    sems = (4, 2, 2, 56, 56, 14, 14, 2, 2, 10, 10, 10, 10, 1, 1, 1, 1, 4, 4, 4, 4, 1, 1, 8, 8, 1, 1)
    return pl.pallas_call(
        kernel,
        out_shape=jax.ShapeDtypeStruct(weight.shape, BF),
        in_specs=[pl.BlockSpec(memory_space=pl.ANY)] * 3,
        out_specs=pl.BlockSpec(memory_space=pltpu.VMEM),
        scratch_shapes=[
            pltpu.VMEM((2048, 512), BF),
            pltpu.VMEM((512, 512), BF),
            pltpu.VMEM((512, 512), jnp.int32),
            pltpu.VMEM((NZ, 2, 2, WIDTH, 1024), BF),
            pltpu.VMEM((NY, NX, 8, 8, 512), F32),
            pltpu.VMEM((NY, NX, 4, 8, 128), F32),
            pltpu.VMEM((NT, 4, 8, 128), F32),
            pltpu.VMEM((2, 4, 4, 8, 8, 256), F32),
            pltpu.VMEM((2, 4, 8, 8, 256), F32),
            pltpu.VMEM((2, 4, 8, 8, 256), F32),
            pltpu.VMEM((8, 8, 512), F32),
            pltpu.VMEM((NZ, 8, 128), F32),
            pltpu.VMEM((2, 32, 128), BF),
            pltpu.VMEM((32, 128), BF),
            pltpu.VMEM((2, 16, 128), BF),
            pltpu.VMEM((NY, NX, 2, 2, 16, 1024), BF),
            pltpu.VMEM((NZ, NT, 8, 1024), F32),
            pltpu.VMEM((ITERS, 1024, 1024), BF),
            pltpu.VMEM((NZ, NY, NX, 8, 512), F32),
            pltpu.VMEM((1024, 512), BF),
            pltpu.VMEM((1024, 512), BF),
            pltpu.VMEM((2, WIDTH, 256), BF),
            pltpu.VMEM((NQ, WIDTH, 256), BF),
            pltpu.VMEM((256, 1024), F32),
            pltpu.VMEM((2, 512, 1024), BF),
            pltpu.VMEM((2, 512, 1024), BF),
        ] + [pltpu.SemaphoreType.DMA((n,)) for n in sems],
        compiler_params=pltpu.CompilerParams(
            collective_id=0, has_side_effects=True, vmem_limit_bytes=56 << 20
        ),
    )(activations, weight, keep_mask)


def solution(mesh):
    return jax.shard_map(
        per_device,
        mesh=mesh,
        in_specs=(P("tok", "col"), P("tok", "col"), P("tok", "col")),
        out_specs=P("tok", "col"),
        check_vma=False,
    )
```
